32 devices in a mesh: dp: 8 (over z, core), tensor: 4 (over y, x).
Axes of the slice: x: 2, y: 2, z: 4, core: 2. Of those that a mesh axis runs over, the one named last changes fastest.
Arguments:
- tokens: bfloat16 [16, 512, 2048], P('dp', 'tensor'), may hold values from -6 to 6
- cotangent: bfloat16 [16, 512, 2048], P('dp', 'tensor'), may hold values from -6 to 6
- lengths: int32 [16], P('dp'), may hold values from 1 to 512, 5120 in all
- attn_gain: float32 [2048], replicated, may hold values from 0.5 to 1.5
- mlp_gain: float32 [2048], replicated, may hold values from 0.5 to 1.5
- w_query: float32 [2048, 2048], P('dp', 'tensor'), may hold values from -0.125 to 0.125
- w_keyval: float32 [2, 2048, 512], P(None, 'dp', 'tensor'), may hold values from -0.125 to 0.125
- w_output: float32 [2048, 2048], P('tensor', 'dp'), may hold values from -1 to 1
- w_gateup: float32 [2, 2048, 8192], P(None, 'dp', 'tensor'), may hold values from -0.125 to 0.125
- w_down: float32 [8192, 2048], P('tensor', 'dp'), may hold values from -0.0625 to 0.0625
- m_attn_gain: float32 [2048], replicated, may hold values from -128 to 128
- m_mlp_gain: float32 [2048], replicated, may hold values from -48 to 48
- m_query: float32 [2048, 2048], P('dp', 'tensor'), may hold values from -96 to 96
- m_keyval: float32 [2, 2048, 512], P(None, 'dp', 'tensor'), may hold values from -128 to 128
- m_output: float32 [2048, 2048], P('tensor', 'dp'), may hold values from -6 to 6
- m_gateup: float32 [2, 2048, 8192], P(None, 'dp', 'tensor'), may hold values from -16 to 16
- m_down: float32 [8192, 2048], P('tensor', 'dp'), may hold values from -48 to 48
- s_attn_gain: float32 [2048], replicated, may hold values from 21.2992 to 335.872
- s_mlp_gain: float32 [2048], replicated, may hold values from 2.359296 to 37.35552
- s_query: float32 [2048, 2048], P('dp', 'tensor'), may hold values from 8.68352 to 137.6256
- s_keyval: float32 [2, 2048, 512], P(None, 'dp', 'tensor'), may hold values from 22.9376 to 360.448
- s_output: float32 [2048, 2048], P('tensor', 'dp'), may hold values from 0.196608 to 3.11296
- s_gateup: float32 [2, 2048, 8192], P(None, 'dp', 'tensor'), may hold values from 0.26624 to 4.3008
- s_down: float32 [8192, 2048], P('tensor', 'dp'), may hold values from 2.12992 to 33.5872
Outputs:
- output: bfloat16 [16, 512, 2048], P('dp', 'tensor')
- input_grad: float32 [16, 512, 2048], P('dp', 'tensor')
- grad_attn_gain: float32 [2048], replicated
- grad_mlp_gain: float32 [2048], replicated
- grad_query: float32 [2048, 2048], P('dp', 'tensor')
- grad_keyval: float32 [2, 2048, 512], P(None, 'dp', 'tensor')
- grad_output: float32 [2048, 2048], P('tensor', 'dp')
- grad_gateup: float32 [2, 2048, 8192], P(None, 'dp', 'tensor')
- grad_down: float32 [8192, 2048], P('tensor', 'dp')
- change_attn_gain: float32 [2048], replicated
- change_mlp_gain: float32 [2048], replicated
- change_query: float32 [2048, 2048], P('dp', 'tensor')
- change_keyval: float32 [2, 2048, 512], P(None, 'dp', 'tensor')
- change_output: float32 [2048, 2048], P('tensor', 'dp')
- change_gateup: float32 [2, 2048, 8192], P(None, 'dp', 'tensor')
- change_down: float32 [8192, 2048], P('tensor', 'dp')
- new_m_attn_gain: float32 [2048], replicated
- new_m_mlp_gain: float32 [2048], replicated
- new_m_query: float32 [2048, 2048], P('dp', 'tensor')
- new_m_keyval: float32 [2, 2048, 512], P(None, 'dp', 'tensor')
- new_m_output: float32 [2048, 2048], P('tensor', 'dp')
- new_m_gateup: float32 [2, 2048, 8192], P(None, 'dp', 'tensor')
- new_m_down: float32 [8192, 2048], P('tensor', 'dp')
- new_s_attn_gain: float32 [2048], replicated
- new_s_mlp_gain: float32 [2048], replicated
- new_s_query: float32 [2048, 2048], P('dp', 'tensor')
- new_s_keyval: float32 [2, 2048, 512], P(None, 'dp', 'tensor')
- new_s_output: float32 [2048, 2048], P('tensor', 'dp')
- new_s_gateup: float32 [2, 2048, 8192], P(None, 'dp', 'tensor')
- new_s_down: float32 [8192, 2048], P('tensor', 'dp')
The draws below stay inside these ranges and needn't reach their ends.
Inputs may be any that keep to these rules, and one draw needn't show every extreme that they name: `lengths`: at least one slot holds 512 real tokens.
All inputs are finite; a program needn't handle non-finite values. No bound on the sum of `lengths` on one device may be relied on, other than what follows from the above.
Results may differ from the reference program's by a relative error of at most 0.02.
Values may be sent and summed in bfloat16 or wider, within the bound.
No kernel may reach another device: no remote copies, remote signals or barrier semaphores. Data moves between devices by JAX's collectives and lax.ppermute only.
A program may use at most 256 MiB of HBM per device.

```python
import math
import jax
import jax.numpy as jnp
import numpy as np
from jax import lax

D = 2048
H = 32
KV = 8
HD = 64
FF = 8192
SEQ_LEN = 512
SEQS = 16


def level_of(own_key, shape, shards, low, largest):
    level, own = 1.0, jax.random.fold_in(own_key, 6)
    for axis_at, parts in shards:
        steps = jnp.exp(jax.random.uniform(jax.random.fold_in(own, axis_at), (parts,), jnp.float32, low / len(shards), largest / len(shards)))
        level = level * jnp.repeat(steps, shape[axis_at] // parts).reshape([-1 if axis == axis_at else 1 for axis in range(len(shape))])
    return level


def split_up(number_of, total, most, lean):
    loads = [(1 << 20) // math.isqrt(rank ** lean) + 1 for rank in range(2, number_of + 1)]
    spare, given = total - most - (number_of - 1), [1] * (number_of - 1)
    while spare > 0:
        free = [i for i in range(number_of - 1) if given[i] < most]
        pool, left = sum([loads[i] for i in free]), spare
        for i in free:
            extra = min(most - given[i], max(1, left * loads[i] // pool), spare)
            given[i] = given[i] + extra
            spare = spare - extra
    return np.array([most] + given)


def ragged(stream_key, amount, total, bound, slope):
    if amount == 2:
        one = jax.random.randint(stream_key, (), max(1, total - bound), min(bound, total - 1) + 1)
        return jnp.stack([one, total - one])
    tallies = jnp.asarray(split_up(amount, total, bound, slope), jnp.int32)
    pairs = (amount - 1) // 2
    source_of, sink = tallies[1:1 + 2 * pairs:2], tallies[2:2 + 2 * pairs:2]
    slack = jnp.minimum(source_of - 1, bound - sink)
    passed = jax.random.randint(jax.random.fold_in(stream_key, 1), (pairs,), 0, 1 << 20) % (slack + 1)
    tallies = tallies.at[1:1 + 2 * pairs:2].set(source_of - passed).at[2:2 + 2 * pairs:2].set(sink + passed)
    return tallies[jax.random.permutation(jax.random.fold_in(stream_key, 2), amount)]


def noise(rng, shape, spread, limit, shards=(), kind=jnp.bfloat16):
    result = spread * jax.random.normal(rng, shape, jnp.float32)
    if shards:
        result = result * level_of(rng, shape, shards, -0.22, 0.18)
    return jnp.clip(result, -limit, limit).astype(kind)


def setup_inputs(seed: int = 0) -> dict:
    splits = jax.random.split(jax.random.key(seed), 25)
    return {
        "tokens": noise(splits[0], (SEQS, SEQ_LEN, D), 1.0, 6.0, ((0, 8), (1, 4))),
        "cotangent": noise(splits[1], (SEQS, SEQ_LEN, D), 1.0, 6.0, ((0, 8), (1, 4))),
        "lengths": ragged(splits[2], SEQS, SEQS * SEQ_LEN * 5 // 8, SEQ_LEN, 2).astype(jnp.int32),
        "attn_gain": jnp.clip(1.0 + 0.1 * jax.random.normal(splits[3], (D,), jnp.float32), 0.5, 1.5),
        "mlp_gain": jnp.clip(1.0 + 0.1 * jax.random.normal(splits[4], (D,), jnp.float32), 0.5, 1.5),
        "w_query": noise(splits[5], (D, H * HD), D ** -0.5, 0.125, ((0, 8), (1, 4)), jnp.float32),
        "w_keyval": noise(splits[6], (2, D, KV * HD), D ** -0.5, 0.125, ((1, 8), (2, 4)), jnp.float32),
        "w_output": noise(splits[7], (H * HD, D), (H * HD // 64) ** -0.5, 1.0, ((0, 4), (1, 8)), jnp.float32),
        "w_gateup": noise(splits[8], (2, D, FF), D ** -0.5, 0.125, ((1, 8), (2, 4)), jnp.float32),
        "w_down": noise(splits[9], (FF, D), FF ** -0.5, 0.0625, ((0, 4), (1, 8)), jnp.float32),
        "m_attn_gain": noise(splits[10], (D,), (0.26 * (SEQS * 512) ** 0.5), 128.0, (), jnp.float32),
        "m_mlp_gain": noise(splits[11], (D,), (0.044 * (SEQS * SEQ_LEN * FF // D) ** 0.5), 48.0, (), jnp.float32),
        "m_query": noise(splits[12], (D, H * HD), (0.17 * (SEQS * 512) ** 0.5), 96.0, ((0, 8), (1, 4)), jnp.float32),
        "m_keyval": noise(splits[13], (2, D, KV * HD), (0.27 * (SEQS * 512) ** 0.5), 128.0, ((1, 8), (2, 4)), jnp.float32),
        "m_output": noise(splits[14], (H * HD, D), (0.026 * (SEQS * 512) ** 0.5), 6.0, ((0, 4), (1, 8)), jnp.float32),
        "m_gateup": noise(splits[15], (2, D, FF), (0.059 * (SEQS * SEQ_LEN * D // FF) ** 0.5), 16.0, ((1, 8), (2, 4)), jnp.float32),
        "m_down": noise(splits[16], (FF, D), (0.083 * (SEQS * SEQ_LEN) ** 0.5), 48.0, ((0, 4), (1, 8)), jnp.float32),
        "s_attn_gain": jnp.clip(jnp.exp(jax.random.uniform(splits[17], (D,), jnp.float32, math.log(21.2992), math.log(335.872))), 21.2992, 335.872),
        "s_mlp_gain": jnp.clip(jnp.exp(jax.random.uniform(splits[18], (D,), jnp.float32, math.log(2.359296), math.log(37.35552))), 2.359296, 37.35552),
        "s_query": jnp.clip(jnp.exp(math.log(137.6256) - 2.76311 * jax.random.uniform(splits[19], (D, H * HD), jnp.float32) ** level_of(splits[19], (D, H * HD), ((0, 8), (1, 4)), -0.2, 0.2)), 8.68352, 137.6256),
        "s_keyval": jnp.clip(jnp.exp(math.log(360.448) - 2.7545702 * jax.random.uniform(splits[20], (2, D, KV * HD), jnp.float32) ** level_of(splits[20], (2, D, KV * HD), ((1, 8), (2, 4)), -0.2, 0.2)), 22.9376, 360.448),
        "s_output": jnp.clip(jnp.exp(math.log(3.11296) - 2.7621174 * jax.random.uniform(splits[21], (H * HD, D), jnp.float32) ** level_of(splits[21], (H * HD, D), ((0, 4), (1, 8)), -0.2, 0.2)), 0.196608, 3.11296),
        "s_gateup": jnp.clip(jnp.exp(math.log(4.3008) - 2.7821581 * jax.random.uniform(splits[22], (2, D, FF), jnp.float32) ** level_of(splits[22], (2, D, FF), ((1, 8), (2, 4)), -0.2, 0.2)), 0.26624, 4.3008),
        "s_down": jnp.clip(jnp.exp(math.log(33.5872) - 2.7580606 * jax.random.uniform(splits[23], (FF, D), jnp.float32) ** level_of(splits[23], (FF, D), ((0, 4), (1, 8)), -0.2, 0.2)), 2.12992, 33.5872),
    }


norm_eps = 1e-05
rope_base = 500000.0
beta_one = 0.9
beta_two = 0.999
learn_rate = 0.003
weight_decay = 0.1
adam_eps = 1e-08
adam_step = 3.0

def rotary_tables(length, half):
    position = jnp.arange(length, dtype=jnp.float32)[:, None]
    freqs = rope_base ** (-(jnp.arange(half, dtype=jnp.float32) / half))
    angle = position * freqs[None, :]
    return (jnp.cos(angle)[:, None, :], jnp.sin(angle)[:, None, :])

def rotate(vectors, cos_table, sin_table):
    half = vectors.shape[-1] // 2
    first_half = vectors[..., :half]
    second_half = vectors[..., half:]
    return jnp.concatenate([first_half * cos_table - second_half * sin_table, second_half * cos_table + first_half * sin_table], -1)

def unrotate(grads_in, cos_table, sin_table):
    half = grads_in.shape[-1] // 2
    first_half = grads_in[..., :half]
    second_half = grads_in[..., half:]
    return jnp.concatenate([first_half * cos_table + second_half * sin_table, second_half * cos_table - first_half * sin_table], -1)

def matmul(left, right):
    return jnp.dot(left, right, preferred_element_type=jnp.float32)

def widen(array):
    return array.astype(jnp.float32)

def adamw(weight, grad, first, second, decay):
    first_new = beta_one * first + (1.0 - beta_one) * grad
    second_new = beta_two * second + (1.0 - beta_two) * grad * grad
    corr_one = 1.0 - beta_one ** adam_step
    corr_two = 1.0 - beta_two ** adam_step
    update = first_new / corr_one / (jnp.sqrt(second_new / corr_two) + adam_eps)
    return (-learn_rate * (update + decay * weight), first_new, second_new)

def reference(tokens, cotangent, lengths, attn_gain, mlp_gain, w_query, w_keyval, w_output, w_gateup, w_down, m_attn_gain, m_mlp_gain, m_query, m_keyval, m_output, m_gateup, m_down, s_attn_gain, s_mlp_gain, s_query, s_keyval, s_output, s_gateup, s_down):
    bf16 = jnp.bfloat16
    f32 = jnp.float32
    group_size = H // KV
    score_scale = HD ** (-0.5)
    query_b = w_query.astype(bf16)
    key_b = w_keyval[0].astype(bf16)
    value_b = w_keyval[1].astype(bf16)
    output_b = w_output.astype(bf16)
    gate_b = w_gateup[0].astype(bf16)
    up_b = w_gateup[1].astype(bf16)
    down_b = w_down.astype(bf16)
    cos_table, sin_table = rotary_tables(SEQ_LEN, HD // 2)
    row_index = jnp.arange(SEQ_LEN, dtype=jnp.int32)[:, None]
    col_index = jnp.arange(SEQ_LEN, dtype=jnp.int32)[None, :]

    def sequence_pass(totals, inputs):
        x_seq, grad_seq, seq_length = inputs
        x_float = x_seq.astype(f32)
        inv_one = lax.rsqrt(lax.optimization_barrier(jnp.mean(x_float * x_float, -1, keepdims=True)) + norm_eps)
        attn_in = (x_float * inv_one * attn_gain).astype(bf16)
        query_rot = rotate(matmul(attn_in, query_b).reshape(SEQ_LEN, H, HD), cos_table, sin_table).astype(bf16)
        key_rot = rotate(matmul(attn_in, key_b).reshape(SEQ_LEN, KV, HD), cos_table, sin_table).astype(bf16)
        values = matmul(attn_in, value_b).reshape(SEQ_LEN, KV, HD).astype(bf16)
        query_grp = query_rot.reshape(SEQ_LEN, KV, group_size, HD)
        allowed = (col_index <= row_index) & (col_index < seq_length)
        scores = jnp.einsum('qkgd,skd->kgqs', widen(query_grp), widen(key_rot)) * score_scale
        masked = jnp.where(allowed, scores, -1e+30)
        row_max = lax.optimization_barrier(jnp.max(masked, -1, keepdims=True))
        log_total = row_max + jnp.log(lax.optimization_barrier(jnp.sum(jnp.exp(masked - row_max), -1, keepdims=True)))
        attn_probs = jnp.exp(jnp.where(allowed, scores - log_total, -1e+30))
        probs_b = attn_probs.astype(bf16)
        mixed = jnp.einsum('kgqs,skd->qkgd', widen(probs_b), widen(values)).astype(bf16)
        mixed_flat = mixed.reshape(SEQ_LEN, H * HD)
        residual = x_float + matmul(mixed_flat, output_b)
        inv_two = lax.rsqrt(lax.optimization_barrier(jnp.mean(residual * residual, -1, keepdims=True)) + norm_eps)
        mlp_in = (residual * inv_two * mlp_gain).astype(bf16)
        gate_proj = matmul(mlp_in, gate_b)
        up_proj = matmul(mlp_in, up_b)
        sigmoid_gate = jax.nn.sigmoid(gate_proj)
        silu_gate = gate_proj * sigmoid_gate
        hidden = (silu_gate * up_proj).astype(bf16)
        block_out = (residual + matmul(hidden, down_b)).astype(bf16)
        live_rows = jnp.arange(SEQ_LEN, dtype=jnp.int32)[:, None] < seq_length
        grad_rows = jnp.where(live_rows, grad_seq, jnp.zeros_like(grad_seq))
        grad_down = matmul(hidden.T, grad_rows)
        grad_hidden = matmul(grad_rows, down_b.T)
        grad_gate = (grad_hidden * up_proj * sigmoid_gate * (1.0 + gate_proj * (1.0 - sigmoid_gate))).astype(bf16)
        grad_up = (grad_hidden * silu_gate).astype(bf16)
        grad_gateup = jnp.stack([matmul(mlp_in.T, grad_gate), matmul(mlp_in.T, grad_up)])
        grad_normed_two = matmul(grad_gate, gate_b.T) + matmul(grad_up, up_b.T)
        scaled_two = mlp_gain * grad_normed_two
        gain_two = lax.optimization_barrier(jnp.sum(grad_normed_two * residual * inv_two, 0))
        grad_resid = grad_rows.astype(f32) + inv_two * scaled_two - residual * inv_two ** 3 * lax.optimization_barrier(jnp.mean(scaled_two * residual, -1, keepdims=True))
        grad_resid_b = grad_resid.astype(bf16)
        grad_out_w = matmul(mixed_flat.T, grad_resid_b)
        grad_mixed = matmul(grad_resid_b, output_b.T).astype(bf16).reshape(SEQ_LEN, KV, group_size, HD)
        grad_probs = jnp.einsum('qkgd,skd->kgqs', widen(grad_mixed), widen(values))
        row_delta = lax.optimization_barrier(jnp.sum(attn_probs * grad_probs, -1, keepdims=True))
        grad_scores = (attn_probs * (grad_probs - row_delta)).astype(bf16)
        grad_values = jnp.einsum('kgqs,qkgd->skd', widen(probs_b), widen(grad_mixed))
        grad_q = jnp.einsum('kgqs,skd->qkgd', widen(grad_scores), widen(key_rot)) * score_scale
        grad_k = jnp.einsum('kgqs,qkgd->skd', widen(grad_scores), widen(query_grp)) * score_scale
        grad_q_b = unrotate(grad_q.reshape(SEQ_LEN, H, HD), cos_table, sin_table).astype(bf16).reshape(SEQ_LEN, H * HD)
        grad_k_b = unrotate(grad_k, cos_table, sin_table).astype(bf16).reshape(SEQ_LEN, KV * HD)
        grad_v_b = grad_values.astype(bf16).reshape(SEQ_LEN, KV * HD)
        grad_query = matmul(attn_in.T, grad_q_b)
        grad_keyval = jnp.stack([matmul(attn_in.T, grad_k_b), matmul(attn_in.T, grad_v_b)])
        grad_normed_one = matmul(grad_q_b, query_b.T) + matmul(grad_k_b, key_b.T) + matmul(grad_v_b, value_b.T)
        scaled_one = attn_gain * grad_normed_one
        gain_one = lax.optimization_barrier(jnp.sum(grad_normed_one * x_float * inv_one, 0))
        input_grad = grad_resid + inv_one * scaled_one - x_float * inv_one ** 3 * lax.optimization_barrier(jnp.mean(scaled_one * x_float, -1, keepdims=True))
        totals = (totals[0] + gain_one, totals[1] + gain_two, totals[2] + grad_query, totals[3] + grad_keyval, totals[4] + grad_out_w, totals[5] + grad_gateup, totals[6] + grad_down)
        return (totals, (block_out, input_grad))
    start = (jnp.zeros((D,), f32), jnp.zeros((D,), f32), jnp.zeros((D, H * HD), f32), jnp.zeros((2, D, KV * HD), f32), jnp.zeros((H * HD, D), f32), jnp.zeros((2, D, FF), f32), jnp.zeros((FF, D), f32))
    totals, outs = lax.scan(sequence_pass, start, (tokens, cotangent, lengths.astype(jnp.int32)))
    output, input_grad = outs
    params = (attn_gain, mlp_gain, w_query, w_keyval, w_output, w_gateup, w_down)
    firsts = (m_attn_gain, m_mlp_gain, m_query, m_keyval, m_output, m_gateup, m_down)
    seconds = (s_attn_gain, s_mlp_gain, s_query, s_keyval, s_output, s_gateup, s_down)
    decays = (0.0, 0.0, weight_decay, weight_decay, weight_decay, weight_decay, weight_decay)
    updated = [adamw(params[idx], totals[idx], firsts[idx], seconds[idx], decays[idx]) for idx in range(7)]
    return (output, input_grad, totals[0], totals[1], totals[2], totals[3], totals[4], totals[5], totals[6], updated[0][0], updated[1][0], updated[2][0], updated[3][0], updated[4][0], updated[5][0], updated[6][0], updated[0][1], updated[1][1], updated[2][1], updated[3][1], updated[4][1], updated[5][1], updated[6][1], updated[0][2], updated[1][2], updated[2][2], updated[3][2], updated[4][2], updated[5][2], updated[6][2])
```

```python
import jax
import jax.numpy as jnp
from jax import lax
from jax.sharding import PartitionSpec as P

HD = 64


norm_eps = 1e-05
rope_base = 500000.0
beta_one = 0.9
beta_two = 0.999
learn_rate = 0.003
weight_decay = 0.1
adam_eps = 1e-08
adam_step = 3.0


def rotary_tables(position, half):
    position = position.astype(jnp.float32)[:, None]
    freqs = rope_base ** (-(jnp.arange(half, dtype=jnp.float32) / half))
    angle = position * freqs[None, :]
    return (jnp.cos(angle)[:, None, :], jnp.sin(angle)[:, None, :])


def rotate(vectors, cos_table, sin_table):
    half = vectors.shape[-1] // 2
    first_half = vectors[..., :half]
    second_half = vectors[..., half:]
    return jnp.concatenate(
        [
            first_half * cos_table - second_half * sin_table,
            second_half * cos_table + first_half * sin_table,
        ],
        -1,
    )


def unrotate(grads_in, cos_table, sin_table):
    half = grads_in.shape[-1] // 2
    first_half = grads_in[..., :half]
    second_half = grads_in[..., half:]
    return jnp.concatenate(
        [
            first_half * cos_table + second_half * sin_table,
            second_half * cos_table - first_half * sin_table,
        ],
        -1,
    )


def swap_pairs(size, step):
    return [(idx, idx ^ step) for idx in range(size)]


def gather_blocks(piece):
    size = lax.axis_size("tensor")
    return [piece] + [
        lax.ppermute(piece, "tensor", swap_pairs(size, step)) for step in range(1, size)
    ]


def scatter_blocks(blocks):
    size = lax.axis_size("tensor")
    total = blocks[0].astype(jnp.float32)
    for step in range(1, size):
        total = total + lax.ppermute(blocks[step], "tensor", swap_pairs(size, step)).astype(
            jnp.float32
        )
    return total


def sum_everywhere(value):
    for axis in ("tensor", "dp"):
        size = lax.axis_size(axis)
        step = 1
        while step < size:
            value = value + lax.ppermute(value, axis, swap_pairs(size, step))
            step = step * 2
    return value


def split_rows(rows):
    size = lax.axis_size("tensor")
    piece = rows.shape[1] // size
    return [rows[:, idx * piece : (idx + 1) * piece] for idx in range(size)]


def attend(query_grp, key_rot, values, allowed, score_scale):
    scores = (
        jnp.einsum("qkgd,skd->kgqs", query_grp, key_rot, preferred_element_type=jnp.float32)
        * score_scale
    )
    masked = jnp.where(allowed, scores, -1e30)
    row_max = jnp.max(masked, -1, keepdims=True)
    log_total = row_max + jnp.log(jnp.sum(jnp.exp(masked - row_max), -1, keepdims=True))
    attn_probs = jnp.exp(jnp.where(allowed, scores - log_total, -1e30))
    probs_b = attn_probs.astype(jnp.bfloat16)
    mixed = jnp.einsum("kgqs,skd->qkgd", probs_b, values, preferred_element_type=jnp.float32)
    return (mixed.astype(jnp.bfloat16), log_total)


def attend_back(query_grp, key_rot, values, log_total, grad_mixed, allowed, score_scale):
    scores = (
        jnp.einsum("qkgd,skd->kgqs", query_grp, key_rot, preferred_element_type=jnp.float32)
        * score_scale
    )
    attn_probs = jnp.exp(jnp.where(allowed, scores - log_total, -1e30))
    probs_b = attn_probs.astype(jnp.bfloat16)
    grad_probs = jnp.einsum(
        "qkgd,skd->kgqs", grad_mixed, values, preferred_element_type=jnp.float32
    )
    row_delta = jnp.sum(attn_probs * grad_probs, -1, keepdims=True)
    grad_scores = (attn_probs * (grad_probs - row_delta)).astype(jnp.bfloat16)
    grad_values = jnp.einsum(
        "kgqs,qkgd->skd", probs_b, grad_mixed, preferred_element_type=jnp.float32
    )
    grad_query = (
        jnp.einsum("kgqs,skd->qkgd", grad_scores, key_rot, preferred_element_type=jnp.float32)
        * score_scale
    )
    grad_keys = (
        jnp.einsum("kgqs,qkgd->skd", grad_scores, query_grp, preferred_element_type=jnp.float32)
        * score_scale
    )
    return (grad_query, grad_keys, grad_values)


def adamw(weight, grad, first, second, decay):
    first_new = beta_one * first + (1.0 - beta_one) * grad
    second_new = beta_two * second + (1.0 - beta_two) * grad * grad
    corr_one = 1.0 - beta_one**adam_step
    corr_two = 1.0 - beta_two**adam_step
    update = first_new / corr_one / (jnp.sqrt(second_new / corr_two) + adam_eps)
    return (-learn_rate * (update + decay * weight), first_new, second_new)


def body(
    tokens,
    cotangent,
    lengths,
    attn_gain,
    mlp_gain,
    w_query,
    w_keyval,
    w_output,
    w_gateup,
    w_down,
    m_attn_gain,
    m_mlp_gain,
    m_query,
    m_keyval,
    m_output,
    m_gateup,
    m_down,
    s_attn_gain,
    s_mlp_gain,
    s_query,
    s_keyval,
    s_output,
    s_gateup,
    s_down,
):
    bf16 = jnp.bfloat16
    f32 = jnp.float32
    seq_here, piece_len, model_width = tokens.shape
    seq_len = piece_len * lax.axis_size("tensor")
    row_count = seq_here * seq_len
    score_scale = HD ** (-0.5)
    q_cols = w_query.shape[1]
    kv_cols = w_keyval.shape[2]
    qkv_cols = q_cols + 2 * kv_cols
    here = lax.axis_index("tensor")
    position = (
        (here ^ jnp.arange(lax.axis_size("tensor"), dtype=jnp.int32))[:, None] * piece_len
        + jnp.arange(piece_len, dtype=jnp.int32)[None, :]
    ).reshape(seq_len)
    cos_table, sin_table = rotary_tables(position, HD // 2)
    attn_shard = jnp.concatenate(
        [
            w_query.astype(bf16),
            w_keyval[0].astype(bf16),
            w_keyval[1].astype(bf16),
            w_output.astype(bf16).T,
        ],
        axis=1,
    )
    attn_full = lax.all_gather(attn_shard, "dp", axis=0, tiled=True)
    gateup_full = lax.all_gather(w_gateup.astype(bf16), "dp", axis=1, tiled=True)
    down_full = lax.all_gather(w_down.astype(bf16), "dp", axis=1, tiled=True)
    qkv_full = attn_full[:, :qkv_cols]
    output_full = attn_full[:, qkv_cols:]
    x_float = tokens.astype(f32)
    inv_one = lax.rsqrt(jnp.mean(x_float * x_float, -1, keepdims=True) + norm_eps)
    normed_one = (x_float * inv_one * attn_gain).astype(bf16)
    attn_in = jnp.concatenate(gather_blocks(normed_one), axis=1).reshape(row_count, model_width)
    live_rows = position[None, :piece_len] < lengths[:, None]
    grad_piece = jnp.where(live_rows[:, :, None], cotangent, jnp.zeros_like(cotangent))
    grad_rows = jnp.concatenate(gather_blocks(grad_piece), axis=1).reshape(row_count, model_width)
    heads_here = q_cols // HD
    kv_here = kv_cols // HD
    group_size = heads_here // kv_here
    qkv_raw = jnp.dot(attn_in, qkv_full, preferred_element_type=f32)
    query_raw = qkv_raw[:, :q_cols].reshape(seq_here, seq_len, heads_here, HD)
    key_raw = qkv_raw[:, q_cols : q_cols + kv_cols].reshape(seq_here, seq_len, kv_here, HD)
    value_raw = qkv_raw[:, q_cols + kv_cols :].reshape(seq_here, seq_len, kv_here, HD)
    query_grp = (
        rotate(query_raw, cos_table, sin_table)
        .astype(bf16)
        .reshape(seq_here, seq_len, kv_here, group_size, HD)
    )
    key_rot = rotate(key_raw, cos_table, sin_table).astype(bf16)
    values = value_raw.astype(bf16)
    causal = position[None, :] <= position[:, None]

    def forward_one(packed):
        allowed = causal & (position[None, :] < packed[3])
        return attend(packed[0], packed[1], packed[2], allowed, score_scale)

    mixed, log_totals = lax.map(forward_one, (query_grp, key_rot, values, lengths))
    mixed_flat = mixed.reshape(row_count, heads_here * HD)
    attn_part = jnp.einsum("rh,dh->rd", mixed_flat, output_full, preferred_element_type=f32)
    attn_total = scatter_blocks(
        split_rows(attn_part.astype(bf16).reshape(seq_here, seq_len, model_width))
    )
    residual = x_float + attn_total
    inv_two = lax.rsqrt(jnp.mean(residual * residual, -1, keepdims=True) + norm_eps)
    normed_two = (residual * inv_two * mlp_gain).astype(bf16)
    mlp_in = jnp.concatenate(gather_blocks(normed_two), axis=1).reshape(row_count, model_width)
    gate_proj = jnp.dot(mlp_in, gateup_full[0], preferred_element_type=f32)
    up_proj = jnp.dot(mlp_in, gateup_full[1], preferred_element_type=f32)
    sigmoid_gate = jax.nn.sigmoid(gate_proj)
    silu_gate = gate_proj * sigmoid_gate
    hidden = (silu_gate * up_proj).astype(bf16)
    mlp_part = jnp.dot(hidden, down_full, preferred_element_type=f32)
    mlp_total = scatter_blocks(
        split_rows(mlp_part.astype(bf16).reshape(seq_here, seq_len, model_width))
    )
    block_out = (residual + mlp_total).astype(bf16)
    grad_down = jnp.einsum("rf,rd->fd", hidden, grad_rows, preferred_element_type=f32)
    grad_hidden = jnp.einsum("rd,fd->rf", grad_rows, down_full, preferred_element_type=f32)
    grad_gate = (
        grad_hidden * up_proj * sigmoid_gate * (1.0 + gate_proj * (1.0 - sigmoid_gate))
    ).astype(bf16)
    grad_up = (grad_hidden * silu_gate).astype(bf16)
    grad_in_two = jnp.einsum(
        "rf,df->rd", grad_gate, gateup_full[0], preferred_element_type=f32
    ) + jnp.einsum("rf,df->rd", grad_up, gateup_full[1], preferred_element_type=f32)
    grad_normed_two = scatter_blocks(
        split_rows(grad_in_two.astype(bf16).reshape(seq_here, seq_len, model_width))
    )
    grad_gate_w = jnp.einsum("rd,rf->df", mlp_in, grad_gate, preferred_element_type=f32)
    grad_up_w = jnp.einsum("rd,rf->df", mlp_in, grad_up, preferred_element_type=f32)
    scaled_two = mlp_gain * grad_normed_two
    gain_two_part = jnp.sum(grad_normed_two * residual * inv_two, axis=(0, 1))
    grad_resid = (
        grad_piece.astype(f32)
        + inv_two * scaled_two
        - residual * inv_two**3 * jnp.mean(scaled_two * residual, -1, keepdims=True)
    )
    grad_resid_b = grad_resid.astype(bf16)
    grad_attn_rows = jnp.concatenate(gather_blocks(grad_resid_b), axis=1).reshape(
        row_count, model_width
    )
    grad_out_w = jnp.einsum("rd,rh->dh", grad_attn_rows, mixed_flat, preferred_element_type=f32)
    grad_mixed = jnp.dot(grad_attn_rows, output_full, preferred_element_type=f32).astype(bf16)
    grad_mixed = grad_mixed.reshape(seq_here, seq_len, kv_here, group_size, HD)

    def backward_one(packed):
        allowed = causal & (position[None, :] < packed[5])
        return attend_back(
            packed[0], packed[1], packed[2], packed[3], packed[4], allowed, score_scale
        )

    grad_q, grad_k, grad_v = lax.map(
        backward_one, (query_grp, key_rot, values, log_totals, grad_mixed, lengths)
    )
    grad_q_b = unrotate(
        grad_q.reshape(seq_here, seq_len, heads_here, HD), cos_table, sin_table
    ).astype(bf16)
    grad_q_b = grad_q_b.reshape(row_count, heads_here * HD)
    grad_k_b = unrotate(grad_k, cos_table, sin_table).astype(bf16).reshape(row_count, kv_here * HD)
    grad_v_b = grad_v.astype(bf16).reshape(row_count, kv_here * HD)
    grad_qkv_b = jnp.concatenate([grad_q_b, grad_k_b, grad_v_b], axis=1)
    grad_qkv_w = jnp.einsum("rd,rh->dh", attn_in, grad_qkv_b, preferred_element_type=f32)
    grad_in_one = jnp.einsum("rh,dh->rd", grad_qkv_b, qkv_full, preferred_element_type=f32)
    grad_normed_one = scatter_blocks(
        split_rows(grad_in_one.astype(bf16).reshape(seq_here, seq_len, model_width))
    )
    scaled_one = attn_gain * grad_normed_one
    gain_one_part = jnp.sum(grad_normed_one * x_float * inv_one, axis=(0, 1))
    input_grad = (
        grad_resid
        + inv_one * scaled_one
        - x_float * inv_one**3 * jnp.mean(scaled_one * x_float, -1, keepdims=True)
    )
    gain_grads = sum_everywhere(jnp.stack([gain_one_part, gain_two_part]))
    grad_down_s = lax.psum_scatter(
        grad_down.astype(bf16), "dp", scatter_dimension=1, tiled=True
    ).astype(f32)
    grad_gate_s = lax.psum_scatter(
        grad_gate_w.astype(bf16), "dp", scatter_dimension=0, tiled=True
    ).astype(f32)
    grad_up_s = lax.psum_scatter(
        grad_up_w.astype(bf16), "dp", scatter_dimension=0, tiled=True
    ).astype(f32)
    grad_attn_s = lax.psum_scatter(
        jnp.concatenate([grad_qkv_w.astype(bf16), grad_out_w.astype(bf16)], axis=1),
        "dp",
        scatter_dimension=0,
        tiled=True,
    ).astype(f32)
    grads_all = (
        gain_grads[0],
        gain_grads[1],
        grad_attn_s[:, :q_cols],
        jnp.stack(
            [grad_attn_s[:, q_cols : q_cols + kv_cols], grad_attn_s[:, q_cols + kv_cols : qkv_cols]]
        ),
        grad_attn_s[:, qkv_cols:].T,
        jnp.stack([grad_gate_s, grad_up_s]),
        grad_down_s,
    )
    params = (attn_gain, mlp_gain, w_query, w_keyval, w_output, w_gateup, w_down)
    firsts = (m_attn_gain, m_mlp_gain, m_query, m_keyval, m_output, m_gateup, m_down)
    seconds = (s_attn_gain, s_mlp_gain, s_query, s_keyval, s_output, s_gateup, s_down)
    decays = (0.0, 0.0, weight_decay, weight_decay, weight_decay, weight_decay, weight_decay)
    updated = [
        adamw(params[idx], grads_all[idx], firsts[idx], seconds[idx], decays[idx])
        for idx in range(7)
    ]
    return (
        block_out,
        input_grad,
        grads_all[0],
        grads_all[1],
        grads_all[2],
        grads_all[3],
        grads_all[4],
        grads_all[5],
        grads_all[6],
        updated[0][0],
        updated[1][0],
        updated[2][0],
        updated[3][0],
        updated[4][0],
        updated[5][0],
        updated[6][0],
        updated[0][1],
        updated[1][1],
        updated[2][1],
        updated[3][1],
        updated[4][1],
        updated[5][1],
        updated[6][1],
        updated[0][2],
        updated[1][2],
        updated[2][2],
        updated[3][2],
        updated[4][2],
        updated[5][2],
        updated[6][2],
    )


def solution(mesh):
    placed = (
        P("dp", "tensor", None),
        P("dp", "tensor", None),
        P("dp"),
        P(),
        P(),
        P("dp", "tensor"),
        P(None, "dp", "tensor"),
        P("tensor", "dp"),
        P(None, "dp", "tensor"),
        P("tensor", "dp"),
        P(),
        P(),
        P("dp", "tensor"),
        P(None, "dp", "tensor"),
        P("tensor", "dp"),
        P(None, "dp", "tensor"),
        P("tensor", "dp"),
        P(),
        P(),
        P("dp", "tensor"),
        P(None, "dp", "tensor"),
        P("tensor", "dp"),
        P(None, "dp", "tensor"),
        P("tensor", "dp"),
    )
    return jax.shard_map(
        body,
        mesh=mesh,
        in_specs=placed,
        out_specs=(
            P("dp", "tensor", None),
            P("dp", "tensor", None),
            P(),
            P(),
            P("dp", "tensor"),
            P(None, "dp", "tensor"),
            P("tensor", "dp"),
            P(None, "dp", "tensor"),
            P("tensor", "dp"),
            P(),
            P(),
            P("dp", "tensor"),
            P(None, "dp", "tensor"),
            P("tensor", "dp"),
            P(None, "dp", "tensor"),
            P("tensor", "dp"),
            P(),
            P(),
            P("dp", "tensor"),
            P(None, "dp", "tensor"),
            P("tensor", "dp"),
            P(None, "dp", "tensor"),
            P("tensor", "dp"),
            P(),
            P(),
            P("dp", "tensor"),
            P(None, "dp", "tensor"),
            P("tensor", "dp"),
            P(None, "dp", "tensor"),
            P("tensor", "dp"),
        ),
        check_vma=False,
    )
```

```python
import jax
import jax.numpy as jnp
from jax import lax
from jax.sharding import PartitionSpec as P


HD = 64


norm_eps = 1e-05
rope_base = 500000.0
beta_one = 0.9
beta_two = 0.999
learn_rate = 0.003
weight_decay = 0.1
adam_eps = 1e-08
adam_step = 3.0


def rotary_tables(position, half):
    position = position.astype(jnp.float32)[:, None]
    freqs = rope_base ** (-(jnp.arange(half, dtype=jnp.float32) / half))
    angle = position * freqs[None, :]
    return (jnp.cos(angle)[:, None, :], jnp.sin(angle)[:, None, :])


def rotate(vectors, cos_table, sin_table):
    half = vectors.shape[-1] // 2
    first_half = vectors[..., :half]
    second_half = vectors[..., half:]
    return jnp.concatenate(
        [
            first_half * cos_table - second_half * sin_table,
            second_half * cos_table + first_half * sin_table,
        ],
        -1,
    )


def unrotate(grads_in, cos_table, sin_table):
    half = grads_in.shape[-1] // 2
    first_half = grads_in[..., :half]
    second_half = grads_in[..., half:]
    return jnp.concatenate(
        [
            first_half * cos_table + second_half * sin_table,
            second_half * cos_table - first_half * sin_table,
        ],
        -1,
    )


def swap_pairs(size, step):
    return [(idx, idx ^ step) for idx in range(size)]


def gather_blocks(piece):
    size = lax.axis_size("tensor")
    return [piece] + [
        lax.ppermute(piece, "tensor", swap_pairs(size, step)) for step in range(1, size)
    ]


def scatter_blocks(blocks):
    size = lax.axis_size("tensor")
    total = blocks[0].astype(jnp.float32)
    for step in range(1, size):
        total = total + lax.ppermute(blocks[step], "tensor", swap_pairs(size, step)).astype(
            jnp.float32
        )
    return total


def sum_everywhere(value):
    for axis in ("tensor", "dp"):
        size = lax.axis_size(axis)
        step = 1
        while step < size:
            value = value + lax.ppermute(value, axis, swap_pairs(size, step))
            step = step * 2
    return value


def over_sequences(func, packed):
    results = [func([leaf[idx] for leaf in packed]) for idx in range(packed[0].shape[0])]
    return [jnp.stack(leaves) for leaves in zip(*results)]


def split_rows(rows):
    size = lax.axis_size("tensor")
    piece = rows.shape[1] // size
    return [rows[:, idx * piece : (idx + 1) * piece] for idx in range(size)]


def attend(query_grp, key_rot, values, allowed, score_scale):
    scores = (
        jnp.einsum("qkgd,skd->kgqs", query_grp, key_rot, preferred_element_type=jnp.float32)
        * score_scale
    )
    masked = jnp.where(allowed, scores, -1e30)
    row_max = jnp.max(masked, -1, keepdims=True)
    log_total = row_max + jnp.log(jnp.sum(jnp.exp(masked - row_max), -1, keepdims=True))
    attn_probs = jnp.exp(jnp.where(allowed, scores - log_total, -1e30))
    probs_b = attn_probs.astype(jnp.bfloat16)
    mixed = jnp.einsum("kgqs,skd->qkgd", probs_b, values, preferred_element_type=jnp.float32)
    return (mixed.astype(jnp.bfloat16), log_total)


def attend_back(query_grp, key_rot, values, log_total, grad_mixed, allowed, score_scale):
    scores = (
        jnp.einsum("qkgd,skd->kgqs", query_grp, key_rot, preferred_element_type=jnp.float32)
        * score_scale
    )
    attn_probs = jnp.exp(jnp.where(allowed, scores - log_total, -1e30))
    probs_b = attn_probs.astype(jnp.bfloat16)
    grad_probs = jnp.einsum(
        "qkgd,skd->kgqs", grad_mixed, values, preferred_element_type=jnp.float32
    )
    row_delta = jnp.sum(attn_probs * grad_probs, -1, keepdims=True)
    grad_scores = (attn_probs * (grad_probs - row_delta)).astype(jnp.bfloat16)
    grad_values = jnp.einsum(
        "kgqs,qkgd->skd", probs_b, grad_mixed, preferred_element_type=jnp.float32
    )
    grad_query = (
        jnp.einsum("kgqs,skd->qkgd", grad_scores, key_rot, preferred_element_type=jnp.float32)
        * score_scale
    )
    grad_keys = (
        jnp.einsum("kgqs,qkgd->skd", grad_scores, query_grp, preferred_element_type=jnp.float32)
        * score_scale
    )
    return (grad_query, grad_keys, grad_values)


def adamw(weight, grad, first, second, decay):
    first_new = beta_one * first + (1.0 - beta_one) * grad
    second_new = beta_two * second + (1.0 - beta_two) * grad * grad
    corr_one = 1.0 - beta_one**adam_step
    corr_two = 1.0 - beta_two**adam_step
    update = first_new / corr_one / (jnp.sqrt(second_new / corr_two) + adam_eps)
    return (-learn_rate * (update + decay * weight), first_new, second_new)


def body(
    tokens,
    cotangent,
    lengths,
    attn_gain,
    mlp_gain,
    w_query,
    w_keyval,
    w_output,
    w_gateup,
    w_down,
    m_attn_gain,
    m_mlp_gain,
    m_query,
    m_keyval,
    m_output,
    m_gateup,
    m_down,
    s_attn_gain,
    s_mlp_gain,
    s_query,
    s_keyval,
    s_output,
    s_gateup,
    s_down,
):
    bf16 = jnp.bfloat16
    f32 = jnp.float32
    seq_here, piece_len, model_width = tokens.shape
    seq_len = piece_len * lax.axis_size("tensor")
    row_count = seq_here * seq_len
    score_scale = HD ** (-0.5)
    q_cols = w_query.shape[1]
    kv_cols = w_keyval.shape[2]
    qkv_cols = q_cols + 2 * kv_cols
    here = lax.axis_index("tensor")
    position = (
        (here ^ jnp.arange(lax.axis_size("tensor"), dtype=jnp.int32))[:, None] * piece_len
        + jnp.arange(piece_len, dtype=jnp.int32)[None, :]
    ).reshape(seq_len)
    cos_table, sin_table = rotary_tables(position, HD // 2)
    attn_shard = jnp.concatenate(
        [
            w_query.astype(bf16),
            w_keyval[0].astype(bf16),
            w_keyval[1].astype(bf16),
            w_output.astype(bf16).T,
        ],
        axis=1,
    )
    attn_full = lax.all_gather(attn_shard, "dp", axis=0, tiled=True)
    gateup_full = lax.all_gather(w_gateup.astype(bf16), "dp", axis=1, tiled=True)
    down_full = lax.all_gather(w_down.astype(bf16), "dp", axis=1, tiled=True)
    qkv_full = attn_full[:, :qkv_cols]
    output_full = attn_full[:, qkv_cols:]
    x_float = tokens.astype(f32)
    inv_one = lax.rsqrt(jnp.mean(x_float * x_float, -1, keepdims=True) + norm_eps)
    normed_one = (x_float * inv_one * attn_gain).astype(bf16)
    attn_in = jnp.concatenate(gather_blocks(normed_one), axis=1).reshape(row_count, model_width)
    live_rows = position[None, :piece_len] < lengths[:, None]
    grad_piece = jnp.where(live_rows[:, :, None], cotangent, jnp.zeros_like(cotangent))
    grad_rows = jnp.concatenate(gather_blocks(grad_piece), axis=1).reshape(row_count, model_width)
    heads_here = q_cols // HD
    kv_here = kv_cols // HD
    group_size = heads_here // kv_here
    qkv_raw = jnp.dot(attn_in, qkv_full, preferred_element_type=f32)
    query_raw = qkv_raw[:, :q_cols].reshape(seq_here, seq_len, heads_here, HD)
    key_raw = qkv_raw[:, q_cols : q_cols + kv_cols].reshape(seq_here, seq_len, kv_here, HD)
    value_raw = qkv_raw[:, q_cols + kv_cols :].reshape(seq_here, seq_len, kv_here, HD)
    query_grp = (
        rotate(query_raw, cos_table, sin_table)
        .astype(bf16)
        .reshape(seq_here, seq_len, kv_here, group_size, HD)
    )
    key_rot = rotate(key_raw, cos_table, sin_table).astype(bf16)
    values = value_raw.astype(bf16)
    causal = position[None, :] <= position[:, None]

    def forward_one(packed):
        allowed = causal & (position[None, :] < packed[3])
        return attend(packed[0], packed[1], packed[2], allowed, score_scale)

    mixed, log_totals = over_sequences(forward_one, (query_grp, key_rot, values, lengths))
    mixed_flat = mixed.reshape(row_count, heads_here * HD)
    attn_part = jnp.einsum("rh,dh->rd", mixed_flat, output_full, preferred_element_type=f32)
    attn_total = scatter_blocks(
        split_rows(attn_part.astype(bf16).reshape(seq_here, seq_len, model_width))
    )
    residual = x_float + attn_total
    inv_two = lax.rsqrt(jnp.mean(residual * residual, -1, keepdims=True) + norm_eps)
    normed_two = (residual * inv_two * mlp_gain).astype(bf16)
    mlp_in = jnp.concatenate(gather_blocks(normed_two), axis=1).reshape(row_count, model_width)
    gate_proj = jnp.dot(mlp_in, gateup_full[0], preferred_element_type=f32)
    up_proj = jnp.dot(mlp_in, gateup_full[1], preferred_element_type=f32)
    sigmoid_gate = jax.nn.sigmoid(gate_proj)
    silu_gate = gate_proj * sigmoid_gate
    hidden = (silu_gate * up_proj).astype(bf16)
    mlp_part = jnp.dot(hidden, down_full, preferred_element_type=f32)
    mlp_total = scatter_blocks(
        split_rows(mlp_part.astype(bf16).reshape(seq_here, seq_len, model_width))
    )
    block_out = (residual + mlp_total).astype(bf16)
    grad_down = jnp.einsum("rf,rd->fd", hidden, grad_rows, preferred_element_type=f32)
    down_send = grad_down.astype(bf16)
    grad_rows_late, _ = lax.optimization_barrier((grad_rows, down_send))
    down_send, _ = lax.optimization_barrier((down_send, down_full))
    grad_down_s = lax.psum_scatter(down_send, "dp", scatter_dimension=1, tiled=True)
    grad_hidden = jnp.einsum("rd,fd->rf", grad_rows_late, down_full, preferred_element_type=f32)
    grad_gate = (
        grad_hidden * up_proj * sigmoid_gate * (1.0 + gate_proj * (1.0 - sigmoid_gate))
    ).astype(bf16)
    grad_up = (grad_hidden * silu_gate).astype(bf16)
    grad_in_two = jnp.einsum(
        "rf,df->rd", grad_gate, gateup_full[0], preferred_element_type=f32
    ) + jnp.einsum("rf,df->rd", grad_up, gateup_full[1], preferred_element_type=f32)
    grad_in_two = grad_in_two.astype(bf16)
    mlp_in_late, _ = lax.optimization_barrier((mlp_in, grad_in_two))
    grad_normed_two = scatter_blocks(
        split_rows(grad_in_two.reshape(seq_here, seq_len, model_width))
    )
    gate_send = jnp.einsum(
        "rd,rf->df", mlp_in_late, grad_gate, preferred_element_type=f32
    ).astype(bf16)
    up_send = jnp.einsum("rd,rf->df", mlp_in_late, grad_up, preferred_element_type=f32).astype(bf16)
    grad_gate_s = lax.psum_scatter(gate_send, "dp", scatter_dimension=0, tiled=True)
    grad_up_s = lax.psum_scatter(up_send, "dp", scatter_dimension=0, tiled=True)
    grad_normed_two, _, _ = lax.optimization_barrier((grad_normed_two, gate_send, up_send))
    scaled_two = mlp_gain * grad_normed_two
    gain_two_part = jnp.sum(grad_normed_two * residual * inv_two, axis=(0, 1))
    grad_resid = (
        grad_piece.astype(f32)
        + inv_two * scaled_two
        - residual * inv_two**3 * jnp.mean(scaled_two * residual, -1, keepdims=True)
    )
    grad_resid_b = grad_resid.astype(bf16)
    grad_attn_rows = jnp.concatenate(gather_blocks(grad_resid_b), axis=1).reshape(
        row_count, model_width
    )
    grad_attn_rows, _ = lax.optimization_barrier((grad_attn_rows, grad_down_s))
    grad_out_w = jnp.einsum("rd,rh->dh", grad_attn_rows, mixed_flat, preferred_element_type=f32)
    grad_mixed = jnp.dot(grad_attn_rows, output_full, preferred_element_type=f32).astype(bf16)
    grad_mixed = grad_mixed.reshape(seq_here, seq_len, kv_here, group_size, HD)

    def backward_one(packed):
        allowed = causal & (position[None, :] < packed[5])
        return attend_back(
            packed[0], packed[1], packed[2], packed[3], packed[4], allowed, score_scale
        )

    grad_q, grad_k, grad_v = over_sequences(
        backward_one, (query_grp, key_rot, values, log_totals, grad_mixed, lengths)
    )
    grad_q_b = unrotate(
        grad_q.reshape(seq_here, seq_len, heads_here, HD), cos_table, sin_table
    ).astype(bf16)
    grad_q_b = grad_q_b.reshape(row_count, heads_here * HD)
    grad_k_b = unrotate(grad_k, cos_table, sin_table).astype(bf16).reshape(row_count, kv_here * HD)
    grad_v_b = grad_v.astype(bf16).reshape(row_count, kv_here * HD)
    grad_qkv_b = jnp.concatenate([grad_q_b, grad_k_b, grad_v_b], axis=1)
    grad_qkv_w = jnp.einsum("rd,rh->dh", attn_in, grad_qkv_b, preferred_element_type=f32)
    grad_in_one = jnp.einsum("rh,dh->rd", grad_qkv_b, qkv_full, preferred_element_type=f32)
    grad_normed_one = scatter_blocks(
        split_rows(grad_in_one.astype(bf16).reshape(seq_here, seq_len, model_width))
    )
    scaled_one = attn_gain * grad_normed_one
    gain_one_part = jnp.sum(grad_normed_one * x_float * inv_one, axis=(0, 1))
    input_grad = (
        grad_resid
        + inv_one * scaled_one
        - x_float * inv_one**3 * jnp.mean(scaled_one * x_float, -1, keepdims=True)
    )
    gain_grads = sum_everywhere(jnp.stack([gain_one_part, gain_two_part]))
    attn_send = jnp.concatenate([grad_qkv_w.astype(bf16), grad_out_w.astype(bf16)], axis=1)
    grad_attn_s = lax.psum_scatter(attn_send, "dp", scatter_dimension=0, tiled=True).astype(f32)
    grad_down_s = grad_down_s.astype(f32)
    grad_gate_s = grad_gate_s.astype(f32)
    grad_up_s = grad_up_s.astype(f32)
    grads_all = (
        gain_grads[0],
        gain_grads[1],
        grad_attn_s[:, :q_cols],
        jnp.stack(
            [grad_attn_s[:, q_cols : q_cols + kv_cols], grad_attn_s[:, q_cols + kv_cols : qkv_cols]]
        ),
        grad_attn_s[:, qkv_cols:].T,
        jnp.stack([grad_gate_s, grad_up_s]),
        grad_down_s,
    )
    params = (attn_gain, mlp_gain, w_query, w_keyval, w_output, w_gateup, w_down)
    firsts = (m_attn_gain, m_mlp_gain, m_query, m_keyval, m_output, m_gateup, m_down)
    seconds = (s_attn_gain, s_mlp_gain, s_query, s_keyval, s_output, s_gateup, s_down)
    decays = (0.0, 0.0, weight_decay, weight_decay, weight_decay, weight_decay, weight_decay)
    updated = [
        adamw(params[idx], grads_all[idx], firsts[idx], seconds[idx], decays[idx])
        for idx in range(7)
    ]
    return (
        block_out,
        input_grad,
        grads_all[0],
        grads_all[1],
        grads_all[2],
        grads_all[3],
        grads_all[4],
        grads_all[5],
        grads_all[6],
        updated[0][0],
        updated[1][0],
        updated[2][0],
        updated[3][0],
        updated[4][0],
        updated[5][0],
        updated[6][0],
        updated[0][1],
        updated[1][1],
        updated[2][1],
        updated[3][1],
        updated[4][1],
        updated[5][1],
        updated[6][1],
        updated[0][2],
        updated[1][2],
        updated[2][2],
        updated[3][2],
        updated[4][2],
        updated[5][2],
        updated[6][2],
    )


def solution(mesh):
    placed = (
        P("dp", "tensor", None),
        P("dp", "tensor", None),
        P("dp"),
        P(),
        P(),
        P("dp", "tensor"),
        P(None, "dp", "tensor"),
        P("tensor", "dp"),
        P(None, "dp", "tensor"),
        P("tensor", "dp"),
        P(),
        P(),
        P("dp", "tensor"),
        P(None, "dp", "tensor"),
        P("tensor", "dp"),
        P(None, "dp", "tensor"),
        P("tensor", "dp"),
        P(),
        P(),
        P("dp", "tensor"),
        P(None, "dp", "tensor"),
        P("tensor", "dp"),
        P(None, "dp", "tensor"),
        P("tensor", "dp"),
    )

    return jax.shard_map(
        body,
        mesh=mesh,
        in_specs=placed,
        out_specs=(
            P("dp", "tensor", None),
            P("dp", "tensor", None),
            P(),
            P(),
            P("dp", "tensor"),
            P(None, "dp", "tensor"),
            P("tensor", "dp"),
            P(None, "dp", "tensor"),
            P("tensor", "dp"),
            P(),
            P(),
            P("dp", "tensor"),
            P(None, "dp", "tensor"),
            P("tensor", "dp"),
            P(None, "dp", "tensor"),
            P("tensor", "dp"),
            P(),
            P(),
            P("dp", "tensor"),
            P(None, "dp", "tensor"),
            P("tensor", "dp"),
            P(None, "dp", "tensor"),
            P("tensor", "dp"),
            P(),
            P(),
            P("dp", "tensor"),
            P(None, "dp", "tensor"),
            P("tensor", "dp"),
            P(None, "dp", "tensor"),
            P("tensor", "dp"),
        ),
        check_vma=False,
    )
```

```python
import jax
import jax.numpy as jnp
from jax import lax
from jax.sharding import PartitionSpec as P


HD = 64


norm_eps = 1e-05
rope_base = 500000.0
beta_one = 0.9
beta_two = 0.999
learn_rate = 0.003
weight_decay = 0.1
adam_eps = 1e-08
adam_step = 3.0


def rotary_tables(position, half):
    position = position.astype(jnp.float32)[:, None]
    freqs = rope_base ** (-(jnp.arange(half, dtype=jnp.float32) / half))
    angle = position * freqs[None, :]
    return (jnp.cos(angle)[:, None, :], jnp.sin(angle)[:, None, :])


def rotate(vectors, cos_table, sin_table):
    half = vectors.shape[-1] // 2
    first_half = vectors[..., :half]
    second_half = vectors[..., half:]
    return jnp.concatenate(
        [
            first_half * cos_table - second_half * sin_table,
            second_half * cos_table + first_half * sin_table,
        ],
        -1,
    )


def unrotate(grads_in, cos_table, sin_table):
    half = grads_in.shape[-1] // 2
    first_half = grads_in[..., :half]
    second_half = grads_in[..., half:]
    return jnp.concatenate(
        [
            first_half * cos_table + second_half * sin_table,
            second_half * cos_table - first_half * sin_table,
        ],
        -1,
    )


def swap_pairs(size, step):
    return [(idx, idx ^ step) for idx in range(size)]


def gather_blocks(piece):
    size = lax.axis_size("tensor")
    return [piece] + [
        lax.ppermute(piece, "tensor", swap_pairs(size, step)) for step in range(1, size)
    ]


def scatter_blocks(blocks):
    size = lax.axis_size("tensor")
    total = blocks[0].astype(jnp.float32)
    for step in range(1, size):
        total = total + lax.ppermute(blocks[step], "tensor", swap_pairs(size, step)).astype(
            jnp.float32
        )
    return total


def sum_everywhere(value):
    for axis in ("tensor", "dp"):
        size = lax.axis_size(axis)
        step = 1
        while step < size:
            value = value + lax.ppermute(value, axis, swap_pairs(size, step))
            step = step * 2
    return value


def over_sequences(func, packed):
    results = [func([leaf[idx] for leaf in packed]) for idx in range(packed[0].shape[0])]
    return [jnp.stack(leaves) for leaves in zip(*results)]


def split_rows(rows):
    size = lax.axis_size("tensor")
    piece = rows.shape[1] // size
    return [rows[:, idx * piece : (idx + 1) * piece] for idx in range(size)]


def attend(query_grp, key_rot, values, allowed, score_scale):
    scores = (
        jnp.einsum("qkgd,skd->kgqs", query_grp, key_rot, preferred_element_type=jnp.float32)
        * score_scale
    )
    masked = jnp.where(allowed, scores, -1e30)
    row_max = jnp.max(masked, -1, keepdims=True)
    log_total = row_max + jnp.log(jnp.sum(jnp.exp(masked - row_max), -1, keepdims=True))
    attn_probs = jnp.exp(jnp.where(allowed, scores - log_total, -1e30))
    probs_b = attn_probs.astype(jnp.bfloat16)
    mixed = jnp.einsum("kgqs,skd->qkgd", probs_b, values, preferred_element_type=jnp.float32)
    return (mixed.astype(jnp.bfloat16), log_total)


def attend_back(query_grp, key_rot, values, log_total, grad_mixed, allowed, score_scale):
    scores = (
        jnp.einsum("qkgd,skd->kgqs", query_grp, key_rot, preferred_element_type=jnp.float32)
        * score_scale
    )
    attn_probs = jnp.exp(jnp.where(allowed, scores - log_total, -1e30))
    probs_b = attn_probs.astype(jnp.bfloat16)
    grad_probs = jnp.einsum(
        "qkgd,skd->kgqs", grad_mixed, values, preferred_element_type=jnp.float32
    )
    row_delta = jnp.sum(attn_probs * grad_probs, -1, keepdims=True)
    grad_scores = (attn_probs * (grad_probs - row_delta)).astype(jnp.bfloat16)
    grad_values = jnp.einsum(
        "kgqs,qkgd->skd", probs_b, grad_mixed, preferred_element_type=jnp.float32
    )
    grad_query = (
        jnp.einsum("kgqs,skd->qkgd", grad_scores, key_rot, preferred_element_type=jnp.float32)
        * score_scale
    )
    grad_keys = (
        jnp.einsum("kgqs,qkgd->skd", grad_scores, query_grp, preferred_element_type=jnp.float32)
        * score_scale
    )
    return (grad_query, grad_keys, grad_values)


def adamw(weight, grad, first, second, decay):
    first_new = beta_one * first + (1.0 - beta_one) * grad
    second_new = beta_two * second + (1.0 - beta_two) * grad * grad
    corr_one = 1.0 - beta_one**adam_step
    corr_two = 1.0 - beta_two**adam_step
    update = first_new / corr_one / (jnp.sqrt(second_new / corr_two) + adam_eps)
    return (-learn_rate * (update + decay * weight), first_new, second_new)


def body(
    tokens,
    cotangent,
    lengths,
    attn_gain,
    mlp_gain,
    w_query,
    w_keyval,
    w_output,
    w_gateup,
    w_down,
    m_attn_gain,
    m_mlp_gain,
    m_query,
    m_keyval,
    m_output,
    m_gateup,
    m_down,
    s_attn_gain,
    s_mlp_gain,
    s_query,
    s_keyval,
    s_output,
    s_gateup,
    s_down,
):
    bf16 = jnp.bfloat16
    f32 = jnp.float32
    seq_here, piece_len, model_width = tokens.shape
    seq_len = piece_len * lax.axis_size("tensor")
    row_count = seq_here * seq_len
    score_scale = HD ** (-0.5)
    q_cols = w_query.shape[1]
    kv_cols = w_keyval.shape[2]
    qkv_cols = q_cols + 2 * kv_cols
    here = lax.axis_index("tensor")
    position = (
        (here ^ jnp.arange(lax.axis_size("tensor"), dtype=jnp.int32))[:, None] * piece_len
        + jnp.arange(piece_len, dtype=jnp.int32)[None, :]
    ).reshape(seq_len)
    cos_table, sin_table = rotary_tables(position, HD // 2)
    attn_shard = jnp.concatenate(
        [
            w_query.astype(bf16),
            w_keyval[0].astype(bf16),
            w_keyval[1].astype(bf16),
            w_output.astype(bf16).T,
        ],
        axis=1,
    )
    attn_full = lax.all_gather(attn_shard, "dp", axis=0, tiled=True)
    gateup_full = lax.all_gather(w_gateup.astype(bf16), "dp", axis=1, tiled=True)
    down_full = lax.all_gather(w_down.astype(bf16), "dp", axis=1, tiled=True)
    qkv_full = attn_full[:, :qkv_cols]
    output_full = attn_full[:, qkv_cols:]
    x_float = tokens.astype(f32)
    inv_one = lax.rsqrt(jnp.mean(x_float * x_float, -1, keepdims=True) + norm_eps)
    normed_one = (x_float * inv_one * attn_gain).astype(bf16)
    attn_in = jnp.concatenate(gather_blocks(normed_one), axis=1).reshape(row_count, model_width)
    live_rows = position[None, :piece_len] < lengths[:, None]
    grad_piece = jnp.where(live_rows[:, :, None], cotangent, jnp.zeros_like(cotangent))
    grad_rows = jnp.concatenate(gather_blocks(grad_piece), axis=1).reshape(row_count, model_width)
    heads_here = q_cols // HD
    kv_here = kv_cols // HD
    group_size = heads_here // kv_here
    qkv_raw = jnp.dot(attn_in, qkv_full, preferred_element_type=f32)
    query_raw = qkv_raw[:, :q_cols].reshape(seq_here, seq_len, heads_here, HD)
    key_raw = qkv_raw[:, q_cols : q_cols + kv_cols].reshape(seq_here, seq_len, kv_here, HD)
    value_raw = qkv_raw[:, q_cols + kv_cols :].reshape(seq_here, seq_len, kv_here, HD)
    query_grp = (
        rotate(query_raw, cos_table, sin_table)
        .astype(bf16)
        .reshape(seq_here, seq_len, kv_here, group_size, HD)
    )
    key_rot = rotate(key_raw, cos_table, sin_table).astype(bf16)
    values = value_raw.astype(bf16)
    causal = position[None, :] <= position[:, None]

    def forward_one(packed):
        allowed = causal & (position[None, :] < packed[3])
        return attend(packed[0], packed[1], packed[2], allowed, score_scale)

    mixed, log_totals = over_sequences(forward_one, (query_grp, key_rot, values, lengths))
    mixed_flat = mixed.reshape(row_count, heads_here * HD)
    attn_part = jnp.einsum("rh,dh->rd", mixed_flat, output_full, preferred_element_type=f32)
    attn_total = scatter_blocks(
        split_rows(attn_part.astype(bf16).reshape(seq_here, seq_len, model_width))
    )
    residual = x_float + attn_total
    inv_two = lax.rsqrt(jnp.mean(residual * residual, -1, keepdims=True) + norm_eps)
    normed_two = (residual * inv_two * mlp_gain).astype(bf16)
    mlp_in = jnp.concatenate(gather_blocks(normed_two), axis=1).reshape(row_count, model_width)
    gate_proj = jnp.dot(mlp_in, gateup_full[0], preferred_element_type=f32)
    up_proj = jnp.dot(mlp_in, gateup_full[1], preferred_element_type=f32)
    sigmoid_gate = jax.nn.sigmoid(gate_proj)
    silu_gate = gate_proj * sigmoid_gate
    hidden = (silu_gate * up_proj).astype(bf16)
    mlp_part = jnp.dot(hidden, down_full, preferred_element_type=f32)
    mlp_total = scatter_blocks(
        split_rows(mlp_part.astype(bf16).reshape(seq_here, seq_len, model_width))
    )
    grad_down = jnp.einsum("rf,rd->fd", hidden, grad_rows, preferred_element_type=f32)
    down_send = grad_down.astype(bf16)
    grad_rows_late, _ = lax.optimization_barrier((grad_rows, down_send))
    down_send, _ = lax.optimization_barrier((down_send, down_full))
    grad_down_s = lax.psum_scatter(down_send, "dp", scatter_dimension=1, tiled=True)
    grad_hidden = jnp.einsum("rd,fd->rf", grad_rows_late, down_full, preferred_element_type=f32)
    grad_gate = (
        grad_hidden * up_proj * sigmoid_gate * (1.0 + gate_proj * (1.0 - sigmoid_gate))
    ).astype(bf16)
    grad_up = (grad_hidden * silu_gate).astype(bf16)
    grad_in_two = jnp.einsum(
        "rf,df->rd", grad_gate, gateup_full[0], preferred_element_type=f32
    ) + jnp.einsum("rf,df->rd", grad_up, gateup_full[1], preferred_element_type=f32)
    grad_in_two = grad_in_two.astype(bf16)
    mlp_in_late, _ = lax.optimization_barrier((mlp_in, grad_in_two))
    grad_normed_two = scatter_blocks(
        split_rows(grad_in_two.reshape(seq_here, seq_len, model_width))
    )
    gate_send = jnp.einsum(
        "rd,rf->df", mlp_in_late, grad_gate, preferred_element_type=f32
    ).astype(bf16)
    up_send = jnp.einsum("rd,rf->df", mlp_in_late, grad_up, preferred_element_type=f32).astype(bf16)
    grad_gate_s = lax.psum_scatter(gate_send, "dp", scatter_dimension=0, tiled=True)
    grad_up_s = lax.psum_scatter(up_send, "dp", scatter_dimension=0, tiled=True)
    grad_normed_two, _, _ = lax.optimization_barrier((grad_normed_two, gate_send, up_send))
    scaled_two = mlp_gain * grad_normed_two
    gain_two_part = jnp.sum(grad_normed_two * residual * inv_two, axis=(0, 1))
    grad_resid = (
        grad_piece.astype(f32)
        + inv_two * scaled_two
        - residual * inv_two**3 * jnp.mean(scaled_two * residual, -1, keepdims=True)
    )
    grad_resid_b = grad_resid.astype(bf16)
    grad_attn_rows = jnp.concatenate(gather_blocks(grad_resid_b), axis=1).reshape(
        row_count, model_width
    )
    new_down = adamw(w_down, grad_down_s.astype(f32), m_down, s_down, weight_decay)
    residual_late, _ = lax.optimization_barrier((residual, grad_attn_rows))
    block_out = (residual_late + mlp_total).astype(bf16)
    grad_attn_rows, _ = lax.optimization_barrier((grad_attn_rows, new_down))
    grad_out_w = jnp.einsum("rd,rh->dh", grad_attn_rows, mixed_flat, preferred_element_type=f32)
    grad_mixed = jnp.dot(grad_attn_rows, output_full, preferred_element_type=f32).astype(bf16)
    grad_mixed = grad_mixed.reshape(seq_here, seq_len, kv_here, group_size, HD)

    def backward_one(packed):
        allowed = causal & (position[None, :] < packed[5])
        return attend_back(
            packed[0], packed[1], packed[2], packed[3], packed[4], allowed, score_scale
        )

    grad_q, grad_k, grad_v = over_sequences(
        backward_one, (query_grp, key_rot, values, log_totals, grad_mixed, lengths)
    )
    grad_q_b = unrotate(
        grad_q.reshape(seq_here, seq_len, heads_here, HD), cos_table, sin_table
    ).astype(bf16)
    grad_q_b = grad_q_b.reshape(row_count, heads_here * HD)
    grad_k_b = unrotate(grad_k, cos_table, sin_table).astype(bf16).reshape(row_count, kv_here * HD)
    grad_v_b = grad_v.astype(bf16).reshape(row_count, kv_here * HD)
    grad_qkv_b = jnp.concatenate([grad_q_b, grad_k_b, grad_v_b], axis=1)
    grad_qkv_w = jnp.einsum("rd,rh->dh", attn_in, grad_qkv_b, preferred_element_type=f32)
    grad_in_one = jnp.einsum("rh,dh->rd", grad_qkv_b, qkv_full, preferred_element_type=f32)
    grad_normed_one = scatter_blocks(
        split_rows(grad_in_one.astype(bf16).reshape(seq_here, seq_len, model_width))
    )
    grad_gateup_s = jnp.stack([grad_gate_s, grad_up_s]).astype(f32)
    new_gateup = adamw(w_gateup, grad_gateup_s, m_gateup, s_gateup, weight_decay)
    grad_normed_one, _ = lax.optimization_barrier((grad_normed_one, new_gateup))
    scaled_one = attn_gain * grad_normed_one
    gain_one_part = jnp.sum(grad_normed_one * x_float * inv_one, axis=(0, 1))
    input_grad = (
        grad_resid
        + inv_one * scaled_one
        - x_float * inv_one**3 * jnp.mean(scaled_one * x_float, -1, keepdims=True)
    )
    gain_grads = sum_everywhere(jnp.stack([gain_one_part, gain_two_part]))
    attn_send = jnp.concatenate([grad_qkv_w.astype(bf16), grad_out_w.astype(bf16)], axis=1)
    grad_attn_s = lax.psum_scatter(attn_send, "dp", scatter_dimension=0, tiled=True).astype(f32)
    grads_all = (
        gain_grads[0],
        gain_grads[1],
        grad_attn_s[:, :q_cols],
        jnp.stack(
            [grad_attn_s[:, q_cols : q_cols + kv_cols], grad_attn_s[:, q_cols + kv_cols : qkv_cols]]
        ),
        grad_attn_s[:, qkv_cols:].T,
        grad_gateup_s,
        grad_down_s.astype(f32),
    )
    params = (attn_gain, mlp_gain, w_query, w_keyval, w_output)
    firsts = (m_attn_gain, m_mlp_gain, m_query, m_keyval, m_output)
    seconds = (s_attn_gain, s_mlp_gain, s_query, s_keyval, s_output)
    decays = (0.0, 0.0, weight_decay, weight_decay, weight_decay)
    updated = [
        adamw(params[idx], grads_all[idx], firsts[idx], seconds[idx], decays[idx])
        for idx in range(5)
    ] + [new_gateup, new_down]
    return (
        block_out,
        input_grad,
        grads_all[0],
        grads_all[1],
        grads_all[2],
        grads_all[3],
        grads_all[4],
        grads_all[5],
        grads_all[6],
        updated[0][0],
        updated[1][0],
        updated[2][0],
        updated[3][0],
        updated[4][0],
        updated[5][0],
        updated[6][0],
        updated[0][1],
        updated[1][1],
        updated[2][1],
        updated[3][1],
        updated[4][1],
        updated[5][1],
        updated[6][1],
        updated[0][2],
        updated[1][2],
        updated[2][2],
        updated[3][2],
        updated[4][2],
        updated[5][2],
        updated[6][2],
    )


def solution(mesh):
    placed = (
        P("dp", "tensor", None),
        P("dp", "tensor", None),
        P("dp"),
        P(),
        P(),
        P("dp", "tensor"),
        P(None, "dp", "tensor"),
        P("tensor", "dp"),
        P(None, "dp", "tensor"),
        P("tensor", "dp"),
        P(),
        P(),
        P("dp", "tensor"),
        P(None, "dp", "tensor"),
        P("tensor", "dp"),
        P(None, "dp", "tensor"),
        P("tensor", "dp"),
        P(),
        P(),
        P("dp", "tensor"),
        P(None, "dp", "tensor"),
        P("tensor", "dp"),
        P(None, "dp", "tensor"),
        P("tensor", "dp"),
    )

    return jax.shard_map(
        body,
        mesh=mesh,
        in_specs=placed,
        out_specs=(
            P("dp", "tensor", None),
            P("dp", "tensor", None),
            P(),
            P(),
            P("dp", "tensor"),
            P(None, "dp", "tensor"),
            P("tensor", "dp"),
            P(None, "dp", "tensor"),
            P("tensor", "dp"),
            P(),
            P(),
            P("dp", "tensor"),
            P(None, "dp", "tensor"),
            P("tensor", "dp"),
            P(None, "dp", "tensor"),
            P("tensor", "dp"),
            P(),
            P(),
            P("dp", "tensor"),
            P(None, "dp", "tensor"),
            P("tensor", "dp"),
            P(None, "dp", "tensor"),
            P("tensor", "dp"),
            P(),
            P(),
            P("dp", "tensor"),
            P(None, "dp", "tensor"),
            P("tensor", "dp"),
            P(None, "dp", "tensor"),
            P("tensor", "dp"),
        ),
        check_vma=False,
    )
```
